256 devices in a mesh: ref: 64 (over z, y_lo, x), win: 4 (over y_hi, core).
Axes of the slice: x: 4, y: 4 (y_hi: 2, y_lo: 2; y = y_hi * 2 + y_lo), z: 8, core: 2. Of those that a mesh axis runs over, the one named last changes fastest.
Arguments:
- queries: bfloat16 [2048, 8192], P('ref', 'win'), may hold values from -1 to 1, as said below
- references: bfloat16 [65536, 8192], P('ref', 'win'), may hold values from -1 to 1, as said below
- labels: int32 [512], P('ref'), may hold values from 0 to 7, as said below
- kernel: float32 [9, 8], replicated, may hold values from 0.02 to 0.3
- class_bias: float32 [8], replicated, may hold values from -4 to 4
Outputs:
- ancestry_logprob: float32 [16, 8, 2048], P('win', None, 'ref')
The draws below stay inside these ranges and needn't reach their ends.
Inputs may be any that keep to these rules, and one draw needn't show every extreme that they name: `queries`: every entry is -1 or +1. `references`: every entry is -1 or +1. Every ancestry labels at least one block.
All inputs are finite; a program needn't handle non-finite values.
Results may differ from the reference program's by a relative error of at most 0.0003.
Values may be sent and summed in bfloat16 or wider, within the bound.
A program may use at most 64 MiB of HBM per device.

```python
import jax
import jax.numpy as jnp
from jax import lax

S = 512
A = 8
BLOCK = 128
TAPS = 9
NQ = 2048
NR = 65536
W = 16
NBLK = 512


def genome_pair(key):
    key_refs = jax.random.fold_in(key, 11)
    key_query = jax.random.fold_in(key, 23)
    key_copy = jax.random.fold_in(key, 37)
    references = (jax.random.randint(key_refs, (NR, W * S), 0, 2) * 2 - 1).astype(jnp.float32)
    queries = (jax.random.randint(key_query, (NQ, W * S), 0, 2) * 2 - 1).astype(jnp.float32)
    copy_count = max(NQ // 8, 1)
    copy_keys = jax.random.split(key_copy, 6)
    copied_rows = jax.random.permutation(copy_keys[0], NQ)[:copy_count]
    source = jax.random.randint(copy_keys[1], (copy_count,), 0, NR // 2) * 2
    twin_rows = source + 1
    window_sites = jnp.arange(S)
    first_site = jax.random.randint(copy_keys[2], (copy_count, W, 1), 0, S)
    flip_mask = (window_sites == first_site).reshape(copy_count, W * S)
    source_rows = references[source]
    references = references.at[twin_rows].set(jnp.where(flip_mask, -source_rows, source_rows))
    levels = jnp.array([0, S // 32, S // 16], dtype=jnp.int32)
    strength = levels[jax.random.randint(copy_keys[4], (copy_count,), 0, 3)]
    noise_mask = jax.random.randint(copy_keys[5], (copy_count, W * S), 0, S) < strength[:, None]
    queries = queries.at[copied_rows].set(jnp.where(noise_mask, -source_rows, source_rows))
    return (references, queries)


def draw_queries(key, part):
    return genome_pair(key)[1].astype(jnp.bfloat16)


def draw_references(key, part):
    return genome_pair(key)[0].astype(jnp.bfloat16)


def draw_labels(key, part):
    key_label = jax.random.fold_in(key, 51)
    key_place = jax.random.fold_in(key, 53)
    labels = jax.random.randint(key_label, (NBLK,), 0, A)
    placed = jax.random.permutation(key_place, NBLK)[:A]
    return labels.at[placed].set(jnp.arange(A, dtype=jnp.int32)).astype(jnp.int32)


def noise(stream_key, extent, deviation, most, kind=jnp.bfloat16):
    values = jax.random.normal(stream_key, extent, jnp.float32) * deviation
    return jnp.minimum(jnp.maximum(values, -most), most).astype(kind)


def setup_inputs(seed: int = 0) -> dict:
    seeds = jax.random.split(jax.random.key(seed), 6)
    return {
        "queries": draw_queries(jax.random.fold_in(seeds[5], 71), 0),
        "references": draw_references(jax.random.fold_in(seeds[5], 71), 0),
        "labels": draw_labels(jax.random.fold_in(seeds[5], 71), 0),
        "kernel": jnp.clip(jax.random.uniform(seeds[3], (TAPS, A), jnp.float32, 0.02, 0.3), 0.02, 0.3),
        "class_bias": noise(seeds[4], (A,), 1.0, 4.0, jnp.float32),
    }


def reference(queries, references, labels, kernel, class_bias):
    owner_label = jnp.repeat(labels, BLOCK)
    score_scale = 256.0 / S

    def pooled_window(window):
        start_col = (window * S).astype(jnp.int32)
        query_part = lax.dynamic_slice_in_dim(queries, start_col, S, 1)
        ref_part = lax.dynamic_slice_in_dim(references, start_col, S, 1)
        scores = jnp.dot(query_part, ref_part.T, preferred_element_type=jnp.float32) * score_scale

        def ancestry_lse(ancestry):
            member = (owner_label == ancestry).astype(scores.dtype)
            return jax.nn.logsumexp(scores, axis=1, b=member[None, :])

        return lax.map(ancestry_lse, jnp.arange(A, dtype=jnp.int32))

    pooled = lax.map(pooled_window, jnp.arange(W, dtype=jnp.int32))
    centered = pooled - jnp.mean(pooled, axis=1, keepdims=True)
    half_width = TAPS // 2
    padded = jnp.pad(centered, ((half_width, half_width), (0, 0), (0, 0)))
    smoothed = jnp.zeros_like(centered)
    for offset in range(TAPS):
        smoothed = smoothed + kernel[offset][None, :, None] * padded[offset:offset + W]
    logits = smoothed + class_bias[None, :, None]
    return jax.nn.log_softmax(logits, axis=1)
```

```python
import math

import jax
import jax.numpy as jnp
from jax import lax
from jax.experimental import pallas as pl
from jax.experimental.pallas import tpu as pltpu
from jax.sharding import PartitionSpec as P

S = 512
A = 8
BLOCK = 128
TAPS = 9

Z, Y, X = 8, 2, 4
PEERS = Z * Y * X
WINDOWS = 4
ROWS = 32
REFS = 1024
BLOCKS = REFS // BLOCK
GROUP = 8
LANES = GROUP * ROWS
GROUPS = PEERS // GROUP
STEPS = GROUPS * WINDOWS

DIRECTIONS = ((1, 0, 0), (-1, 0, 0), (0, 0, 1), (0, 0, -1), (0, 1, 0))

SCHEDULE = (
    (64, 128, 192, 0, 128),
    (0, 0, 64, 128, 0),
    (192, 192, 128, 192, 64),
    (128, 64, 0, 64, 192),
    (72, 184, 72, 3, 3),
    (193, 56, 193, 132, 72),
    (132, 248, 65, 131, 193),
    (8, 120, 132, 68, 8),
    (200, 193, 8, 196, 200),
    (129, 65, 68, 248, 1),
    (136, 129, 56, 120, 56),
    (80, 131, 176, 56, 248),
    (7, 132, 48, 80, 120),
    (135, 240, 240, 76, 48),
    (16, 48, 112, 204, 240),
    (208, 176, 201, 208, 176),
    (144, 112, 9, 16, 112),
    (66, 251, 137, 144, 208),
    (12, 187, 177, 48, 80),
    (140, 123, 49, 15, 88),
    (83, 241, 241, 143, 24),
    (88, 177, 113, 79, 202),
    (216, 49, 104, 216, 216),
    (152, 40, 152, 24, 152),
    (147, 243, 88, 211, 40),
    (10, 180, 24, 40, 178),
    (138, 116, 216, 104, 232),
    (74, 179, 212, 91, 50),
    (14, 114, 148, 28, 242),
    (78, 178, 84, 220, 114),
    (206, 242, 20, 156, 91),
    (142, 50, 153, 219, 235),
    (18, 182, 172, 172, 43),
    (182, 54, 236, 108, 105),
    (54, 246, 44, 96, 106),
    (246, 235, 32, 32, 90),
    (118, 169, 96, 160, 160),
    (214, 44, 224, 159, 96),
    (220, 239, 28, 31, 153),
    (213, 174, 92, 124, 121),
    (95, 46, 190, 252, 249),
    (94, 238, 60, 190, 59),
    (154, 47, 33, 99, 163),
    (239, 234, 180, 180, 33),
    (45, 237, 100, 52, 115),
    (237, 95, 164, 118, 147),
    (207, 25, 140, 20, 85),
    (69, 217, 204, 14, 149),
    (254, 2, 121, 7, 190),
    (126, 83, 10, 251, 130),
    (195, -1, -1, 136, -1),
)

RESIDENCE = 3
SLOT_US = 0.70
STEP_US = 0.65
ISSUE_AHEAD_US = 1.4
ARRIVAL_US = 1.9

LOG2_E = math.log2(math.e)
SCALE = 256.0 / S
NEG_FLOOR = -1e30
MESH = pl.DeviceIdType.MESH


def moved(offset, step):
    z, y, x = offset // (Y * X), offset // X % Y, offset % X
    return ((z + step[0]) % Z * Y + (y + step[1]) % Y) * X + (x + step[2]) % X


def make_plan():
    arrival = {}
    for time, row in enumerate(SCHEDULE):
        for step, piece in zip(DIRECTIONS, row):
            if piece >= 0:
                window, offset = divmod(piece, PEERS)
                arrival[window, moved(offset, step)] = time
    assert len(arrival) == WINDOWS * (PEERS - 1)
    rank = {
        offset: (
            max(arrival[w, offset] for w in range(WINDOWS)),
            sum(arrival[w, offset] for w in range(WINDOWS)),
            offset,
        )
        for offset in range(1, PEERS)
    }
    order = [0] + sorted(rank, key=rank.get)
    ready = []
    for step in range(STEPS):
        group, window = divmod(step, WINDOWS)
        members = order[group * GROUP : (group + 1) * GROUP]
        last = max(arrival[window, o] for o in members if o)
        ready.append((last + 1) * SLOT_US + ARRIVAL_US)
    before = []
    now, time = 0.0, 0
    for step in range(STEPS):
        sends = []
        while True:
            due = time * SLOT_US - ISSUE_AHEAD_US if time < len(SCHEDULE) else 1e9
            if due <= now or due <= ready[step]:
                if due > now and ready[step] <= now:
                    break
                now = max(now, due)
                sends.append(time)
                time += 1
                continue
            break
        now = max(now, ready[step]) + STEP_US
        before.append(sends)
    before.append(list(range(time, len(SCHEDULE))))
    return order, before


def kernel_body(
    queries, references, labels, taps, bias, out,
    qbuf, rbuf, scores, pooled_part, result, inbox, halo, centred,
    own_sem, ref_sem, send_sem, recv_sem, result_send, result_recv,
    halo_send, halo_recv,
):
    order, before = make_plan()
    slot_of = {offset: slot for slot, offset in enumerate(order)}

    me = lax.axis_index("ref")
    win = lax.axis_index("win")
    mz, my, mx = me // (Y * X), me // X % Y, me % X

    def peer(step):
        z = lax.rem(mz + (step[0] + Z), Z)
        y = lax.rem(my + (step[1] + Y), Y)
        x = lax.rem(mx + (step[2] + X), X)
        return (z * Y + y) * X + x

    neighbours = [peer(step) for step in DIRECTIONS]
    sides = [lax.rem(win + 3, 4), lax.rem(win + 1, 4)]

    def own_copy(window):
        return pltpu.make_async_copy(
            queries.at[:, pl.ds(window * S, S)],
            qbuf.at[window, pl.ds(0, ROWS), :],
            own_sem.at[window],
        )

    def ref_copy(window):
        return pltpu.make_async_copy(
            references.at[:, pl.ds(window * S, S)], rbuf.at[window], ref_sem.at[window]
        )

    def piece_ref(window, offset):
        return qbuf.at[window, pl.ds(slot_of[offset] * ROWS, ROWS), :]

    def piece_copy(window, offset, direction):
        landing = moved(offset, DIRECTIONS[direction])
        return pltpu.make_async_remote_copy(
            src_ref=piece_ref(window, offset),
            dst_ref=piece_ref(window, landing),
            send_sem=send_sem.at[direction],
            recv_sem=recv_sem.at[window, slot_of[landing]],
            device_id={"ref": neighbours[direction]},
            device_id_type=MESH,
        )

    def arrived(window, offset):
        ref = piece_ref(window, offset)
        pltpu.make_async_remote_copy(
            src_ref=ref,
            dst_ref=ref,
            send_sem=send_sem.at[0],
            recv_sem=recv_sem.at[window, slot_of[offset]],
            device_id={"ref": neighbours[0]},
            device_id_type=MESH,
        ).wait_recv()

    def result_copy(slot):
        offset = order[slot]
        z, y, x = offset // (Y * X), offset // X % Y, offset % X
        return pltpu.make_async_remote_copy(
            src_ref=result.at[slot],
            dst_ref=inbox.at[slot],
            send_sem=result_send,
            recv_sem=result_recv,
            device_id={"ref": peer((-z, -y, -x))},
            device_id_type=MESH,
        )

    def halo_copy(side):
        return pltpu.make_async_remote_copy(
            src_ref=centred,
            dst_ref=halo.at[side],
            send_sem=halo_send.at[side],
            recv_sem=halo_recv.at[side],
            device_id={"win": sides[side]},
            device_id_type=MESH,
        )

    for window in range(WINDOWS):
        own_copy(window).start()
    barrier = pltpu.get_barrier_semaphore()
    for neighbour in neighbours:
        pl.semaphore_signal(
            barrier, inc=1, device_id={"ref": neighbour}, device_id_type=MESH
        )
    for side in sides:
        pl.semaphore_signal(barrier, inc=1, device_id={"win": side}, device_id_type=MESH)
    for window in range(WINDOWS):
        ref_copy(window).start()
    for window in range(WINDOWS):
        own_copy(window).wait()
    pl.semaphore_wait(barrier, len(neighbours) + len(sides))

    waited = {(window, 0) for window in range(WINDOWS)}

    def need(actions, window, offset):
        if (window, offset) not in waited:
            waited.add((window, offset))
            actions.append(("arrived", window, offset))

    def sends(actions, times):
        for time in times:
            for direction, piece in enumerate(SCHEDULE[time]):
                if piece >= 0:
                    window, offset = divmod(piece, PEERS)
                    need(actions, window, offset)
                    actions.append(("send", window, offset, direction))

    program = []
    for step in range(STEPS):
        group, window = divmod(step, WINDOWS)
        actions = []
        sends(actions, before[step])
        if step >= WINDOWS and window == 1:
            for slot in range((group - 1) * GROUP, group * GROUP):
                if slot:
                    actions.append(("result", slot))
        if group == 0:
            actions.append(("refs", window))
        for offset in order[group * GROUP : (group + 1) * GROUP]:
            need(actions, window, offset)
        program.append(actions)
    last = []
    sends(last, before[STEPS])
    for slot in range((GROUPS - 1) * GROUP, GROUPS * GROUP):
        last.append(("result", slot))

    def run(actions):
        for kind, *rest in actions:
            if kind == "arrived":
                arrived(*rest)
            elif kind == "send":
                piece_copy(*rest).start()
            elif kind == "result":
                result_copy(*rest).start()
            else:
                ref_copy(*rest).wait()

    row_of = lax.broadcasted_iota(jnp.int32, (A, LANES), 0)
    lane_window = lax.broadcasted_iota(jnp.int32, (A, 128), 1) // ROWS

    def select_actions(step, low, high):
        if high - low == 1:
            run(program[low])
            return
        middle = (low + high) // 2

        @pl.when(step < middle)
        def _():
            select_actions(step, low, middle)

        @pl.when(step >= middle)
        def _():
            select_actions(step, middle, high)

    def pool(group, window):
        query = qbuf[window, pl.ds(pl.multiple_of(group * LANES, LANES), LANES), :]
        scores[...] = lax.dot_general(
            rbuf[window], query, (((1,), (1,)), ((), ())),
            preferred_element_type=jnp.float32,
        )
        peaks, totals = [], []
        for block in range(BLOCKS):
            part = scores[block * BLOCK : (block + 1) * BLOCK, :]
            peak = jnp.max(part, axis=0, keepdims=True)
            peaks.append(peak)
            totals.append(
                jnp.sum(
                    jnp.exp2((part - peak) * (SCALE * LOG2_E)), axis=0, keepdims=True
                )
            )
        member = [row_of == labels[block] for block in range(BLOCKS)]
        group_peak = jnp.full((A, LANES), NEG_FLOOR, jnp.float32)
        for block in range(BLOCKS):
            group_peak = jnp.maximum(
                group_peak, jnp.where(member[block], peaks[block], NEG_FLOOR)
            )
        group_total = jnp.zeros((A, LANES), jnp.float32)
        for block in range(BLOCKS):
            power = jnp.where(
                member[block], (peaks[block] - group_peak) * (SCALE * LOG2_E), NEG_FLOOR
            )
            group_total = group_total + totals[block] * jnp.exp2(power)
        pooled_part[window] = jnp.where(
            group_total > 0, group_peak * SCALE + jnp.log(group_total), NEG_FLOOR
        )

    def collect(group):
        for member in range(GROUP):
            half, place = divmod(member, 128 // ROWS)
            tile = jnp.zeros((A, 128), jnp.float32)
            for window in range(WINDOWS):
                value = pooled_part[window, :, half * 128 : (half + 1) * 128]
                shift = (window - place) * ROWS % 128
                if shift:
                    value = pltpu.roll(value, shift, 1)
                tile = jnp.where(lane_window == window, value, tile)
            result[group * GROUP + member] = tile

    def body(step, carry):
        group, window = step // WINDOWS, step % WINDOWS
        select_actions(step, 0, STEPS)
        pool(group, window)

        @pl.when(window == WINDOWS - 1)
        def _():
            collect(group)

        return carry

    lax.fori_loop(0, STEPS, body, 0)
    run(last)

    pltpu.make_async_remote_copy(
        src_ref=inbox.at[pl.ds(1, PEERS - 1)],
        dst_ref=inbox.at[pl.ds(1, PEERS - 1)],
        send_sem=result_send,
        recv_sem=result_recv,
        device_id={"ref": neighbours[0]},
        device_id_type=MESH,
    ).wait_recv()
    inbox[0] = result[0]
    gathered = inbox[...]
    peak = jnp.max(gathered, axis=0)
    pooled = peak + jnp.log(jnp.sum(jnp.exp(gathered - peak[None]), axis=0))
    own = pooled - jnp.mean(pooled, axis=0, keepdims=True)
    centred[...] = own
    for side in range(2):
        halo_copy(side).start()

    row = row_of[:, :128]

    def column(read):
        tile = jnp.zeros((A, 128), jnp.float32)
        for ancestry in range(A):
            tile = jnp.where(row == ancestry, read(ancestry), tile)
        return tile

    weights = [column(lambda a, t=tap: taps[t, a]) for tap in range(TAPS)]
    offset_tile = column(lambda a: bias[a])

    for side in range(2):
        halo_copy(side).wait_recv()
    upper = jnp.where(win < 3, halo[0], 0.0)
    lower = jnp.where(win > 0, halo[1], 0.0)
    smoothed = jnp.zeros((A, 128), jnp.float32)
    for tap in range(TAPS):
        shift = tap - TAPS // 2
        if shift == 0:
            value = own
        elif abs(shift) == WINDOWS:
            value = upper if shift > 0 else lower
        else:
            amount = -shift * ROWS % 128
            inside = (lane_window + shift >= 0) & (lane_window + shift < WINDOWS)
            value = jnp.where(
                inside,
                pltpu.roll(own, amount, 1),
                pltpu.roll(upper if shift > 0 else lower, amount, 1),
            )
        smoothed = smoothed + weights[tap] * value
    logits = smoothed + offset_tile
    shifted = logits - jnp.max(logits, axis=0, keepdims=True)
    final = shifted - jnp.log(jnp.sum(jnp.exp(shifted), axis=0, keepdims=True))
    for window in range(WINDOWS):
        out[window] = final[:, window * ROWS : (window + 1) * ROWS]

    for direction in range(len(DIRECTIONS)):
        count = sum(row[direction] >= 0 for row in SCHEDULE)
        sent = qbuf.at[0, pl.ds(0, count * ROWS), :]
        pltpu.make_async_remote_copy(
            src_ref=sent,
            dst_ref=sent,
            send_sem=send_sem.at[direction],
            recv_sem=recv_sem.at[0, 0],
            device_id={"ref": neighbours[direction]},
            device_id_type=MESH,
        ).wait_send()
    pltpu.make_async_remote_copy(
        src_ref=result.at[pl.ds(1, PEERS - 1)],
        dst_ref=result.at[pl.ds(1, PEERS - 1)],
        send_sem=result_send,
        recv_sem=result_recv,
        device_id={"ref": neighbours[0]},
        device_id_type=MESH,
    ).wait_send()
    for side in range(2):
        halo_copy(side).wait_send()


def per_device(queries, references, labels, kernel, class_bias):
    hbm = pl.BlockSpec(memory_space=pl.ANY)
    smem = pl.BlockSpec(memory_space=pltpu.SMEM)
    return pl.pallas_call(
        kernel_body,
        out_shape=jax.ShapeDtypeStruct((WINDOWS, A, ROWS), jnp.float32),
        in_specs=[hbm, hbm, smem, smem, smem],
        out_specs=pl.BlockSpec(memory_space=pltpu.VMEM),
        scratch_shapes=[
            pltpu.VMEM((WINDOWS, PEERS * ROWS, S), jnp.bfloat16),
            pltpu.VMEM((WINDOWS, REFS, S), jnp.bfloat16),
            pltpu.VMEM((REFS, LANES), jnp.float32),
            pltpu.VMEM((WINDOWS, A, LANES), jnp.float32),
            pltpu.VMEM((PEERS, A, 128), jnp.float32),
            pltpu.VMEM((PEERS, A, 128), jnp.float32),
            pltpu.VMEM((2, A, 128), jnp.float32),
            pltpu.VMEM((A, 128), jnp.float32),
            pltpu.SemaphoreType.DMA((WINDOWS,)),
            pltpu.SemaphoreType.DMA((WINDOWS,)),
            pltpu.SemaphoreType.DMA((len(DIRECTIONS),)),
            pltpu.SemaphoreType.DMA((WINDOWS, PEERS)),
            pltpu.SemaphoreType.DMA,
            pltpu.SemaphoreType.DMA,
            pltpu.SemaphoreType.DMA((2,)),
            pltpu.SemaphoreType.DMA((2,)),
        ],
        compiler_params=pltpu.CompilerParams(collective_id=0, has_side_effects=True),
        name="ancestry",
    )(queries, references, labels, kernel, class_bias)


def solution(mesh):
    in_specs = (P("ref", "win"), P("ref", "win"), P("ref"), P(), P())
    out_specs = P("win", None, "ref")
    return jax.shard_map(
        per_device, mesh=mesh, in_specs=in_specs, out_specs=out_specs, check_vma=False
    )
```
